512 devices in a mesh: ctx: 32 (over y_lo, z), grp: 16 (over y_hi, x, core).
Axes of the slice: x: 4, y: 4 (y_hi: 2, y_lo: 2; y = y_hi * 2 + y_lo), z: 16, core: 2. Of those that a mesh axis runs over, the one named last changes fastest.
Arguments:
- queries: bfloat16 [16, 16384, 512], P('grp', 'ctx'), as said below
- keys: bfloat16 [16, 16384, 512], P('grp', 'ctx'), as said below
- values: bfloat16 [16, 16384, 512], P('grp', 'ctx'), may hold values from -6 to 6
- summary_pos: int32 [16, 32, 8], P('grp', 'ctx'), may hold values from 0 to 511, as said below
Outputs:
- attended: bfloat16 [16, 16384, 512], P('grp', 'ctx')
The draws below stay inside these ranges and needn't reach their ends.
Inputs may be any that keep to these rules, and one draw needn't show every extreme that they name: queries' entries lie within -320 and 320. keys' entries lie within -6 and 6. `summary_pos`: in each block the j-th summary position lies in [j * 64, (j + 1) * 64); the last one is 511.
All inputs are finite; a program needn't handle non-finite values.
Results may differ from the reference program's by a relative error of at most 0.0045.
Values may be sent and summed in bfloat16 or wider, within the bound.
No kernel may reach another device: no remote copies, remote signals or barrier semaphores. Data moves between devices by JAX's collectives and lax.ppermute only.
A program may use at most 64 MiB of HBM per device.

```python
import math
import jax
import jax.numpy as jnp
from jax import lax

H = 8
HD = 64
W = 512
BLK = 512
SUMM = 8
NG = 16
ROWB = 32
LCTX = 16384


def shared_keys(key):
    base_keys = jnp.clip(jax.random.normal(jax.random.fold_in(key, 11), (NG, LCTX, W), jnp.float32), -6.0, 6.0)
    return base_keys


def draw_keys(key, part):
    base_keys = shared_keys(key)
    result = base_keys
    return result.astype(jnp.bfloat16)


def draw_queries(key, part):
    noise = 2.0 * jnp.clip(jax.random.normal(jax.random.fold_in(key, 13), (NG, LCTX, W), jnp.float32), -6.0, 6.0)
    result = noise
    return result.astype(jnp.bfloat16)


def draw_summary_pos(key, part):
    spacing = BLK // SUMM
    offsets = jax.random.randint(key, (NG, ROWB, SUMM), 0, spacing, jnp.int32)
    slot_index = jnp.arange(SUMM, dtype=jnp.int32)
    offsets = jnp.where(slot_index[None, None, :] == SUMM - 1, spacing - 1, offsets)
    return (slot_index[None, None, :] * spacing + offsets).astype(jnp.int32)


def steps_of(rng, extent, shards, least, high):
    factor_of = 1.0
    for position, parts in shards:
        steps = jax.random.uniform(jax.random.fold_in(jax.random.fold_in(rng, 6), position), (parts,), jnp.float32, least / len(shards), high / len(shards))
        factor_of = factor_of * jnp.repeat(jnp.exp(steps), extent[position] // parts).reshape((-1,) + (1,) * (len(extent) - 1 - position))
    return factor_of


def bell_draw(stream_key, shape, scale, bound, pieces=(), kind=jnp.bfloat16):
    gain = steps_of(stream_key, shape, pieces, -0.22, 0.18) if pieces else 1.0
    array = jax.random.normal(stream_key, shape, jnp.float32) * scale * gain
    return jnp.minimum(jnp.maximum(array, -bound), bound).astype(kind)


def setup_inputs(seed: int = 0) -> dict:
    arg_keys = jax.random.split(jax.random.key(seed), 5)
    return {
        "queries": draw_queries(jax.random.fold_in(arg_keys[4], 71), 0),
        "keys": draw_keys(jax.random.fold_in(arg_keys[4], 71), 0),
        "values": bell_draw(arg_keys[2], (NG, LCTX, W), 1.0, 6.0, ((0, 16), (1, 32))),
        "summary_pos": draw_summary_pos(jax.random.fold_in(arg_keys[4], 71), 0),
    }


masked_score = -1e+30

def reference(queries, keys, values, summary_pos):
    total_tokens = NG * LCTX
    block_count = total_tokens // BLK
    score_scale = 1.0 / math.sqrt(HD)
    query_all = queries.reshape(total_tokens, H, HD)
    key_all = keys.reshape(total_tokens, H, HD)
    value_all = values.reshape(total_tokens, H, HD)
    positions = summary_pos.reshape(block_count, SUMM)
    picked = (jnp.arange(block_count, dtype=jnp.int32)[:, None] * BLK + positions).reshape(-1).astype(jnp.int32)
    summary_keys = key_all[picked].astype(jnp.float32)
    summary_vals = value_all[picked].astype(jnp.float32)
    summary_block = jnp.repeat(jnp.arange(block_count, dtype=jnp.int32), SUMM)
    padding = jnp.zeros((BLK, H, HD), jnp.bfloat16)
    key_padded = jnp.concatenate([padding, key_all], axis=0)
    value_padded = jnp.concatenate([padding, value_all], axis=0)
    window_index = jnp.arange(2 * BLK, dtype=jnp.int32)
    query_index = jnp.arange(BLK, dtype=jnp.int32)

    def one_block(block):
        start_row = (block * BLK).astype(jnp.int32)
        query_rows = lax.dynamic_slice_in_dim(query_all, start_row, BLK, 0).astype(jnp.float32)
        near_keys = lax.dynamic_slice_in_dim(key_padded, start_row, 2 * BLK, 0).astype(jnp.float32)
        near_vals = lax.dynamic_slice_in_dim(value_padded, start_row, 2 * BLK, 0).astype(jnp.float32)
        near_scores = jnp.einsum('qhd,khd->hqk', query_rows, near_keys) * score_scale
        far_scores = jnp.einsum('qhd,rhd->hqr', query_rows, summary_keys) * score_scale
        own_part = (window_index[None, :] >= BLK) & (window_index[None, :] - BLK <= query_index[:, None])
        prev_part = (window_index[None, :] < BLK) & (block >= 1)
        near_mask = (own_part | prev_part)[None]
        far_mask = (summary_block <= block - 2)[None, None, :]
        near_scores = jnp.where(near_mask, near_scores, masked_score)
        far_scores = jnp.where(far_mask, far_scores, masked_score)
        top_score = jnp.maximum(near_scores.max(-1), far_scores.max(-1))
        near_weight = jnp.where(near_mask, jnp.exp(near_scores - top_score[..., None]), 0.0)
        far_weight = jnp.where(far_mask, jnp.exp(far_scores - top_score[..., None]), 0.0)
        weight_total = near_weight.sum(-1) + far_weight.sum(-1)
        near_low = lax.optimization_barrier(near_weight.astype(jnp.bfloat16)).astype(jnp.float32)
        far_low = lax.optimization_barrier(far_weight.astype(jnp.bfloat16)).astype(jnp.float32)
        numer = jnp.einsum('hqk,khd->qhd', near_low, near_vals) + jnp.einsum('hqr,rhd->qhd', far_low, summary_vals)
        result = numer / jnp.transpose(weight_total)[:, :, None]
        return result.astype(jnp.bfloat16).reshape(BLK, H * HD)
    outputs = lax.map(one_block, jnp.arange(block_count, dtype=jnp.int32))
    return outputs.reshape(NG, LCTX, H * HD)
```

```python
import functools
import math

import jax
import jax.numpy as jnp
from jax import lax
from jax.experimental import pallas as pl
from jax.experimental.pallas import tpu as pltpu
from jax.sharding import PartitionSpec as P

H = 8
HD = 64
BLK = 512
SUMM = 8
HALF = 256
ACC = 80
SEND = 72
RATE = math.log2(math.e) / math.sqrt(HD)
FLOOR = -1e29
NONE = -1e30
bf16 = jnp.bfloat16
f32 = jnp.float32


def dot(a, b):
    return lax.dot_general(a, b, (((1,), (0,)), ((), ())), preferred_element_type=f32)


def fold(parts, values_t, peak, acc):
    top = peak
    for part in parts:
        top = jnp.maximum(top, part.max(0, keepdims=True))
    weights = [jnp.exp2((part - top) * RATE).astype(bf16) for part in parts]
    rescale = jnp.exp2((peak - top) * RATE)
    acc = acc * rescale + dot(values_t, jnp.concatenate(weights, axis=0))
    return top, acc


def prep_kernel(pos_ref, q_ref, k_ref, v_ref, send_ref, kv_ref):
    kv_ref[:, : H * HD] = k_ref[...]
    kv_ref[:, H * HD :] = v_ref[...]
    slot = lax.broadcasted_iota(jnp.int32, (16, BLK), 0)
    token = lax.broadcasted_iota(jnp.int32, (16, BLK), 1)
    wanted = jnp.full((16, BLK), -1, jnp.int32)
    for j in range(SUMM):
        wanted = jnp.where(slot == j, pos_ref[j], wanted)
    pick = jnp.where(token == wanted, 1.0, 0.0).astype(bf16)
    k_rows = dot(pick, k_ref[...])[:SUMM]
    v_rows = dot(pick, v_ref[...])[:SUMM]
    blank = jnp.zeros((SUMM, HALF - 128), f32)
    q_t = q_ref[...].T
    for h in range(H):
        part = slice(h * HD, (h + 1) * HD)
        rows = jnp.concatenate([v_rows[:, part], k_rows[:, part], blank], axis=1).astype(bf16)
        for half in range(2):
            send_ref[2 * h + half, :HD] = q_t[part, half * HALF : (half + 1) * HALF]
            send_ref[2 * h + half, HD:] = rows


def spread_kernel(where_ref, got_ref, out_ref):
    odd = where_ref[1] > 0
    pieces = [jnp.where(odd, got_ref[2 * i + 1], got_ref[2 * i]) for i in range(8)]
    rows = jnp.concatenate(pieces, axis=0)
    for z in range(out_ref.shape[0]):
        out_ref[z] = rows


def near_kernel(own, has_ref, qt_ref, *rest):
    if own:
        k_ref, v_ref, acc_ref, peak_ref, vt_ref = rest
        v_t = v_ref[...].T
    else:
        k_ref, acc_in, peak_in, acc_ref, peak_ref, vt_ref = rest
        v_t = k_ref[:, H * HD :].T
    for h in range(H):
        vt_ref[h, :HD] = v_t[h * HD : (h + 1) * HD]
        vt_ref[h, HD:] = jnp.ones((ACC - HD, BLK), bf16)
    zeros = jnp.zeros((HD, HALF), bf16)
    key_at = lax.broadcasted_iota(jnp.int32, (HALF, HALF), 0)
    query_at = lax.broadcasted_iota(jnp.int32, (HALF, HALF), 1)
    causal = key_at <= query_at
    for h in range(H):
        pair = slice((h // 2) * 128, (h // 2 + 1) * 128)
        for half in range(2):
            cols = slice(half * HALF, (half + 1) * HALF)
            q_t = qt_ref[2 * h + half, :HD]
            q_t = jnp.concatenate([q_t, zeros] if h % 2 == 0 else [zeros, q_t], axis=0)
            if own:
                count = (half + 1) * HALF
                parts = [dot(k_ref[i : i + HALF, pair], q_t) for i in range(0, count, HALF)]
                parts[-1] = jnp.where(causal, parts[-1], NONE)
                peak = jnp.full((1, HALF), FLOOR, f32)
                acc = jnp.zeros((ACC, HALF), f32)
            else:
                count = BLK
                parts = [dot(k_ref[i : i + HALF, pair], q_t) for i in range(0, count, HALF)]
                peak = peak_in[h, :1, cols]
                acc = acc_in[h, :, cols]
            new_peak, new_acc = fold(parts, vt_ref[h, :, :count], peak, acc)
            if not own:
                has = has_ref[0] > 0
                new_peak = jnp.where(has, new_peak, peak)
                new_acc = jnp.where(has, new_acc, acc)
            acc_ref[h, :, cols] = new_acc
            peak_ref[h, :, cols] = jnp.broadcast_to(new_peak, (8, HALF))


def far_kernel(where_ref, q_ref, s00_ref, s01_ref, s10_ref, s11_ref, out_ref, vt_ref, k_ref, qt_ref, even_ref, odd_ref):
    c = where_ref[0]
    half = where_ref[1]
    y = c // 16
    sets = (s00_ref, s01_ref, s10_ref, s11_ref)
    part = 256
    tile = 4 * part
    wide = 2 * HALF
    lane = lax.broadcasted_iota(jnp.int32, (part, 128), 1)
    row = lax.broadcasted_iota(jnp.int32, (part, 128), 0)
    age = 64 * ((row % 16) // SUMM) + row // 16 - 32 * lane
    age = jnp.where(lane < 16, age, -(1 << 20))
    key_lane = lane >= HD
    for p in range(4):
        for i, ref in enumerate(sets):
            rows = ref[:, p * 16 : p * 16 + 16].reshape(part, 128)
            start = 128 * p + 32 * (half ^ (i % 2)) + 16 * (y ^ (i // 2))
            bias = jnp.where(age <= c - 2 - start, 0.0, NONE).astype(bf16)
            k_ref[p, i * part : (i + 1) * part] = jnp.where(key_lane, rows, bias)
            vt_ref[p, :, i * part : (i + 1) * part] = rows.T[:ACC]
        vt_ref[p, HD:] = jnp.ones((ACC - HD, tile), bf16)
    at = lax.broadcasted_iota(jnp.int32, (HD, HALF), 0)
    for g in range(16):
        one_hot = jnp.where(at == g, 1.0, 0.0).astype(bf16)
        cols = slice((g % 2) * HALF, (g % 2 + 1) * HALF)
        qt_ref[g // 2, :, cols] = jnp.concatenate([one_hot, q_ref[g, :HD]], axis=0)

    def scores(pair, p, buf, peak):
        for i in range(4):
            piece = dot(k_ref[p, i * part : (i + 1) * part], qt_ref[pair])
            buf[p, i * part : (i + 1) * part] = piece
            peak = jnp.maximum(peak, piece.reshape(part // 8, 8, wide).max(0))
        return peak

    def values(p, buf, top, acc):
        weights = [
            jnp.exp2((buf[p, i * part : (i + 1) * part] - top) * RATE).astype(bf16)
            for i in range(4)
        ]
        return acc + dot(vt_ref[p], jnp.concatenate(weights, axis=0))

    def finish(pair, top, acc):
        total = acc[HD : HD + 1]
        some = total > 0.0
        safe = jnp.where(some, total, 1.0)
        result = (acc[:HD] * (1.0 / safe)).astype(bf16)
        level = jnp.where(some, top * RATE + jnp.log2(safe), NONE)
        high = level.astype(bf16)
        rest = level - high.astype(f32)
        mid = rest.astype(bf16)
        low = (rest - mid.astype(f32)).astype(bf16)
        stats = jnp.concatenate([high, mid, low, jnp.zeros((SEND - HD - 3, wide), bf16)], axis=0)
        for j in range(2):
            cols = slice(j * HALF, (j + 1) * HALF)
            out_ref[2 * pair + j, :HD] = result[:, cols]
            out_ref[2 * pair + j, HD:] = stats[:, cols]

    floor = jnp.full((8, wide), FLOOR, f32)
    empty = jnp.zeros((ACC, wide), f32)

    def turn(pair, count, more, this, other, peak):
        top = peak.max(0, keepdims=True)
        later = jnp.minimum(pair + 1, 7)

        def both(p, carry):
            acc, ahead = carry
            ahead = scores(later, p, other, ahead)
            acc = values(p, this, top, acc)
            return acc, ahead

        acc, ahead = lax.fori_loop(0, count, both, (empty, floor))
        if more:
            ahead = scores(later, jnp.minimum(count, 3), other, ahead)
        finish(pair, top, acc)
        return ahead

    def quad(i, peak):
        peak = turn(2 * i, i + 1, False, even_ref, odd_ref, peak)
        return turn(2 * i + 1, i + 1, True, odd_ref, even_ref, peak)

    lax.fori_loop(0, 4, quad, scores(0, 0, even_ref, floor))


def merge_kernel(acc_ref, peak_ref, far_ref, out_ref):
    for h in range(H):
        columns = []
        for half in range(2):
            cols = slice(half * HALF, (half + 1) * HALF)
            far = far_ref[2 * h + half]
            stats = far[HD:].astype(f32)
            level = stats[0:1] + (stats[1:2] + stats[2:3])
            near = peak_ref[h, :1, cols] * RATE
            top = jnp.maximum(near, level)
            near = jnp.exp2(near - top)
            level = jnp.exp2(level - top)
            total = acc_ref[h, HD : HD + 1, cols] * near + level
            result = acc_ref[h, :HD, cols] * (near / total) + far[:HD].astype(f32) * (level / total)
            columns.append(result)
        wide = jnp.concatenate(columns, axis=1).astype(bf16)
        if h % 2 == 0:
            first = wide
        else:
            both = jnp.concatenate([first, wide], axis=0)
            out_ref[:, (h // 2) * 128 : (h // 2 + 1) * 128] = both.T


def vmem(count):
    return [pl.BlockSpec(memory_space=pltpu.VMEM)] * count


SMEM = pl.BlockSpec(memory_space=pltpu.SMEM)


LIMIT = pltpu.CompilerParams(vmem_limit_bytes=24 << 20)


def cost(flops, size, exps=0):
    return pl.CostEstimate(flops=flops, bytes_accessed=size, transcendentals=exps)


def near(own, has, *args):
    shapes = (
        jax.ShapeDtypeStruct((H, ACC, BLK), f32),
        jax.ShapeDtypeStruct((H, 8, BLK), f32),
    )
    return pl.pallas_call(
        functools.partial(near_kernel, own),
        out_shape=shapes,
        in_specs=[SMEM] + vmem(len(args)),
        out_specs=tuple(vmem(2)),
        scratch_shapes=[pltpu.VMEM((H, ACC, BLK), bf16)],
        compiler_params=LIMIT,
        cost_estimate=cost(2 * H * BLK * BLK * 256, 4 << 20, H * BLK * BLK),
        name="near_own" if own else "near_prev",
    )(has, *args)


def shards(queries, keys, values, summary_pos):
    c = lax.axis_index("ctx")
    g = lax.axis_index("grp")
    groups, per_group = lax.axis_size("grp"), lax.axis_size("ctx")
    layers = per_group // 2
    same_y = [[y * layers + z for z in range(layers)] for y in range(2)]
    other_y = [(i, (i + layers) % per_group) for i in range(per_group)]
    other_core = [(i, i ^ 1) for i in range(groups)]
    q, k, v = queries[0], keys[0], values[0]

    where = jnp.stack([c, g % 2]).astype(jnp.int32)
    has = jnp.where(c + g > 0, 1, 0).astype(jnp.int32)[None]
    send, kv = pl.pallas_call(
        prep_kernel,
        out_shape=(
            jax.ShapeDtypeStruct((groups, SEND, HALF), bf16),
            jax.ShapeDtypeStruct((BLK, 2 * H * HD), bf16),
        ),
        in_specs=[SMEM] + vmem(3),
        out_specs=tuple(vmem(2)),
        cost_estimate=cost(4 * 16 * BLK * BLK, 3 << 20),
        name="prep",
    )(summary_pos[0, 0], q, k, v)
    carried = near(True, has, send, k, v)

    got = lax.all_to_all(send, "grp", 0, 0, tiled=True)
    mine = pl.pallas_call(
        spread_kernel,
        out_shape=jax.ShapeDtypeStruct((layers, 64, 128), bf16),
        grid=(1,),
        in_specs=[SMEM, pl.BlockSpec((groups, SUMM, 128), lambda i: (0, HD // SUMM, 0))],
        out_specs=pl.BlockSpec((layers, 64, 128), lambda i: (0, 0, 0)),
        compiler_params=LIMIT,
        name="spread",
    )(where, got)
    s00 = lax.all_to_all(mine, "ctx", 0, 0, tiled=True, axis_index_groups=same_y)
    s10 = lax.ppermute(s00, "ctx", other_y)
    s01 = lax.ppermute(s00, "grp", other_core)
    s11 = lax.ppermute(s10, "grp", other_core)

    kv, unused = lax.optimization_barrier((kv, s00))
    flat = [t * groups + s for s in range(groups) for t in range(per_group)]
    kv_prev = lax.ppermute(kv, ("ctx", "grp"), list(zip(flat[:-1], flat[1:])))

    partial = pl.pallas_call(
        far_kernel,
        out_shape=jax.ShapeDtypeStruct((groups, SEND, HALF), bf16),
        in_specs=[SMEM] + vmem(5),
        out_specs=vmem(1)[0],
        scratch_shapes=[
            pltpu.VMEM((4, ACC, 1024), bf16),
            pltpu.VMEM((4, 1024, 128), bf16),
            pltpu.VMEM((groups // 2, 128, 2 * HALF), bf16),
            pltpu.VMEM((4, 1024, 2 * HALF), f32),
            pltpu.VMEM((4, 1024, 2 * HALF), f32),
        ],
        compiler_params=pltpu.CompilerParams(vmem_limit_bytes=32 << 20),
        cost_estimate=cost(2 * 40 * 1024 * HALF * 256, 3 << 20, 40 * 1024 * HALF),
        name="far",
    )(where, got, s00, s01, s10, s11)
    far = lax.all_to_all(partial, "grp", 0, 0, tiled=True)
    acc, peak = near(False, has, send, kv_prev, *carried)

    out = pl.pallas_call(
        merge_kernel,
        out_shape=jax.ShapeDtypeStruct((BLK, H * HD), bf16),
        in_specs=vmem(3),
        out_specs=vmem(1)[0],
        compiler_params=LIMIT,
        cost_estimate=cost(H * BLK * HD * 8, 3 << 20),
        name="merge",
    )(acc, peak, far)
    return out[None]


def solution(mesh):
    placed = P("grp", "ctx", None)
    return jax.shard_map(
        shards, mesh=mesh, in_specs=(placed,) * 4, out_specs=placed, check_vma=False
    )
```

```python
import functools
import math

import jax
import jax.numpy as jnp
from jax import lax
from jax.experimental import pallas as pl
from jax.experimental.pallas import tpu as pltpu
from jax.sharding import PartitionSpec as P


H = 8
HD = 64
BLK = 512
SUMM = 8
HALF = 256
ACC = 80
SEND = 72
RATE = math.log2(math.e) / math.sqrt(HD)
FLOOR = -1e29
NONE = -1e30
bf16 = jnp.bfloat16
f32 = jnp.float32


def dot(a, b):
    return lax.dot_general(a, b, (((1,), (0,)), ((), ())), preferred_element_type=f32)


def fold(parts, values_t, peak, acc):
    top = peak
    for part in parts:
        top = jnp.maximum(top, part.max(0, keepdims=True))
    weights = [jnp.exp2((part - top) * RATE).astype(bf16) for part in parts]
    rescale = jnp.exp2((peak - top) * RATE)
    acc = acc * rescale + dot(values_t, jnp.concatenate(weights, axis=0))
    return top, acc


def thirds(value):
    high = value.astype(bf16)
    rest = value - high.astype(f32)
    mid = rest.astype(bf16)
    return high, mid, (rest - mid.astype(f32)).astype(bf16)


def prep_kernel(pos_ref, q_ref, k_ref, v_ref, send_ref):
    slot = lax.broadcasted_iota(jnp.int32, (16, BLK), 0)
    token = lax.broadcasted_iota(jnp.int32, (16, BLK), 1)
    wanted = jnp.full((16, BLK), -1, jnp.int32)
    for j in range(SUMM):
        wanted = jnp.where(slot == j, pos_ref[j], wanted)
    pick = jnp.where(token == wanted, 1.0, 0.0).astype(bf16)
    k_rows = dot(pick, k_ref[...])[:SUMM]
    v_rows = dot(pick, v_ref[...])[:SUMM]
    blank = jnp.zeros((SUMM, HALF - 128), f32)
    q_t = q_ref[...].T
    for h in range(H):
        part = slice(h * HD, (h + 1) * HD)
        rows = jnp.concatenate([v_rows[:, part], k_rows[:, part], blank], axis=1).astype(bf16)
        for half in range(2):
            send_ref[2 * h + half, :HD] = q_t[part, half * HALF : (half + 1) * HALF]
            send_ref[2 * h + half, HD:] = rows


def pick_kernel(where_ref, got_ref, out_ref):
    odd = where_ref[1] > 0
    pieces = [jnp.where(odd, got_ref[2 * i + 1], got_ref[2 * i]) for i in range(8)]
    rows = jnp.concatenate(pieces, axis=0)
    for z in range(out_ref.shape[0]):
        out_ref[z] = rows


def near_kernel(own, has_ref, qt_ref, *rest):
    if own:
        k_ref, v_ref, acc_ref, peak_ref, kv_ref, vt_ref = rest
        kv_ref[:, : H * HD] = k_ref[...]
        kv_ref[:, H * HD :] = v_ref[...]
        v_t = v_ref[...].T
    else:
        k_ref, acc_in, peak_in, acc_ref, peak_ref, vt_ref = rest
        v_t = k_ref[:, H * HD :].T
    for h in range(H):
        vt_ref[h, :HD] = v_t[h * HD : (h + 1) * HD]
        vt_ref[h, HD:] = jnp.ones((ACC - HD, BLK), bf16)
    zeros = jnp.zeros((HD, HALF), bf16)
    key_at = lax.broadcasted_iota(jnp.int32, (HALF, HALF), 0)
    query_at = lax.broadcasted_iota(jnp.int32, (HALF, HALF), 1)
    causal = key_at <= query_at
    for h in range(H):
        pair = slice((h // 2) * 128, (h // 2 + 1) * 128)
        for half in range(2):
            cols = slice(half * HALF, (half + 1) * HALF)
            q_t = qt_ref[2 * h + half, :HD]
            q_t = jnp.concatenate([q_t, zeros] if h % 2 == 0 else [zeros, q_t], axis=0)
            if own:
                count = (half + 1) * HALF
                parts = [dot(k_ref[i : i + HALF, pair], q_t) for i in range(0, count, HALF)]
                parts[-1] = jnp.where(causal, parts[-1], NONE)
                peak = jnp.full((1, HALF), FLOOR, f32)
                acc = jnp.zeros((ACC, HALF), f32)
            else:
                count = BLK
                parts = [dot(k_ref[i : i + HALF, pair], q_t) for i in range(0, count, HALF)]
                peak = peak_in[h, :1, cols]
                acc = acc_in[h, :, cols]
            new_peak, new_acc = fold(parts, vt_ref[h, :, :count], peak, acc)
            if not own:
                has = has_ref[0] > 0
                new_peak = jnp.where(has, new_peak, peak)
                new_acc = jnp.where(has, new_acc, acc)
            acc_ref[h, :, cols] = new_acc
            peak_ref[h, :, cols] = jnp.broadcast_to(new_peak, (8, HALF))


def far_kernel(where_ref, q_ref, s00_ref, s01_ref, s10_ref, s11_ref, out_ref, vt_ref, k_ref, qt_ref, even_ref, odd_ref):
    c = where_ref[0]
    half = where_ref[1]
    y = c // 16
    sets = (s00_ref, s01_ref, s10_ref, s11_ref)
    part = 128
    tile = 4 * part
    wide = 2 * HALF
    lane = lax.broadcasted_iota(jnp.int32, (part, 128), 1)
    layer = lax.broadcasted_iota(jnp.int32, (part, 128), 0) // SUMM
    low = lane < HD
    shift = jnp.where(lane < 16, 32 * lane, 1 << 20)
    ages = []
    for hh in range(2):
        turned = jnp.where((half ^ hh) > 0, layer ^ 8, layer)
        ages.append(turned - shift)
    for gg in range(8):
        for i, ref in enumerate(sets):
            at = slice(i * part, (i + 1) * part)
            rows = ref[:, gg * SUMM : (gg + 1) * SUMM].reshape(part, 128)
            start = 64 * gg + 32 * (half ^ (i % 2)) + 16 * (y ^ (i // 2))
            bias = jnp.where(ages[i % 2] <= c - 2 - start, 0.0, NONE).astype(bf16)
            k_ref[gg, at] = jnp.where(low, bias, rows)
            vt_ref[gg, :, at] = rows.T[:ACC]
        vt_ref[gg, HD:] = jnp.ones((ACC - HD, tile), bf16)
    at = lax.broadcasted_iota(jnp.int32, (HD, HALF), 0)
    for g in range(16):
        one_hot = jnp.where(at == g, 1.0, 0.0).astype(bf16)
        cols = slice((g % 2) * HALF, (g % 2 + 1) * HALF)
        qt_ref[g // 2, :, cols] = jnp.concatenate([one_hot, q_ref[g, :HD]], axis=0)

    def scores(pair, first, count, buf, peak):
        for j in range(count):
            for i in range(0, tile, 256):
                piece = dot(k_ref[first + j, i : i + 256], qt_ref[pair])
                buf[first + j, i : i + 256] = piece
                peak = jnp.maximum(peak, piece.reshape(32, 8, wide).max(0))
        return peak

    def values(first, count, buf, top, acc):
        weights = [
            jnp.exp2((buf[first + j, i : i + 256] - top) * RATE).astype(bf16)
            for j in range(count)
            for i in range(0, tile, 256)
        ]
        rows = [vt_ref[first + j] for j in range(count)]
        return acc + dot(jnp.concatenate(rows, axis=1), jnp.concatenate(weights, axis=0))

    def finish(pair, top, acc):
        total = acc[HD : HD + 1]
        some = total > 0.0
        safe = jnp.where(some, total, 1.0)
        result = (acc[:HD] * (1.0 / safe)).astype(bf16)
        level = jnp.where(some, top * RATE + jnp.log2(safe), NONE)
        stats = jnp.concatenate([*thirds(level), jnp.zeros((SEND - HD - 3, wide), bf16)], axis=0)
        for j in range(2):
            cols = slice(j * HALF, (j + 1) * HALF)
            out_ref[2 * pair + j, :HD] = result[:, cols]
            out_ref[2 * pair + j, HD:] = stats[:, cols]

    floor = jnp.full((8, wide), FLOOR, f32)
    empty = jnp.zeros((ACC, wide), f32)

    def turn(pair, tiles, this, other, peak):
        top = peak.max(0, keepdims=True)
        later = jnp.minimum(pair + 1, 7)

        def both(p, carry):
            acc, ahead = carry
            ahead = scores(later, 2 * p, 2, other, ahead)
            acc = values(2 * p, 2, this, top, acc)
            return acc, ahead

        return later, top, *lax.fori_loop(0, tiles, both, (empty, floor))

    def quad(i, peak):
        later, top, acc, ahead = turn(2 * i, i, even_ref, odd_ref, peak)
        ahead = scores(later, 2 * i, 2, odd_ref, ahead)
        acc = values(2 * i, 1, even_ref, top, acc)
        finish(2 * i, top, acc)
        later, top, acc, ahead = turn(2 * i + 1, i + 1, odd_ref, even_ref, ahead)
        ahead = scores(later, jnp.minimum(2 * i + 2, 7), 1, even_ref, ahead)
        finish(2 * i + 1, top, acc)
        return ahead

    lax.fori_loop(0, 4, quad, scores(0, 0, 1, even_ref, floor))


def merge_kernel(acc_ref, peak_ref, far_ref, out_ref):
    for h in range(H):
        columns = []
        for half in range(2):
            cols = slice(half * HALF, (half + 1) * HALF)
            far = far_ref[2 * h + half]
            stats = far[HD:].astype(f32)
            level = stats[0:1] + (stats[1:2] + stats[2:3])
            near = peak_ref[h, :1, cols] * RATE
            top = jnp.maximum(near, level)
            near = jnp.exp2(near - top)
            level = jnp.exp2(level - top)
            total = acc_ref[h, HD : HD + 1, cols] * near + level
            result = acc_ref[h, :HD, cols] * (near / total) + far[:HD].astype(f32) * (level / total)
            columns.append(result)
        wide = jnp.concatenate(columns, axis=1).astype(bf16)
        if h % 2 == 0:
            first = wide
        else:
            both = jnp.concatenate([first, wide], axis=0)
            out_ref[:, (h // 2) * 128 : (h // 2 + 1) * 128] = both.T


def vmem(count):
    return [pl.BlockSpec(memory_space=pltpu.VMEM)] * count


SMEM = pl.BlockSpec(memory_space=pltpu.SMEM)


LIMIT = pltpu.CompilerParams(vmem_limit_bytes=24 << 20)


def cost(flops, size, exps=0):
    return pl.CostEstimate(flops=flops, bytes_accessed=size, transcendentals=exps)


def near(own, has, *args):
    shapes = (
        jax.ShapeDtypeStruct((H, ACC, BLK), f32),
        jax.ShapeDtypeStruct((H, 8, BLK), f32),
    )
    if own:
        shapes += (jax.ShapeDtypeStruct((BLK, 2 * H * HD), bf16),)
    return pl.pallas_call(
        functools.partial(near_kernel, own),
        out_shape=shapes,
        in_specs=[SMEM] + vmem(len(args)),
        out_specs=tuple(vmem(len(shapes))),
        scratch_shapes=[pltpu.VMEM((H, ACC, BLK), bf16)],
        compiler_params=LIMIT,
        cost_estimate=cost(2 * H * BLK * BLK * 256, 4 << 20, H * BLK * BLK),
        name="near_own" if own else "near_prev",
    )(has, *args)


def shards(queries, keys, values, summary_pos):
    c = lax.axis_index("ctx")
    g = lax.axis_index("grp")
    groups, per_group = lax.axis_size("grp"), lax.axis_size("ctx")
    layers = per_group // 2
    rings = [
        [(y * layers + (z + layers // 2 * (i % 2)) % layers) * groups + i for z in range(layers)]
        for y in range(2)
        for i in range(groups)
    ]
    other_y = [(i, (i + layers) % per_group) for i in range(per_group)]
    other_core = [(i, i ^ 1) for i in range(groups)]
    q, k, v = queries[0], keys[0], values[0]

    where = jnp.stack([c, g % 2]).astype(jnp.int32)
    has = jnp.where(c + g > 0, 1, 0).astype(jnp.int32)[None]
    send = pl.pallas_call(
        prep_kernel,
        out_shape=jax.ShapeDtypeStruct((groups, SEND, HALF), bf16),
        in_specs=[SMEM] + vmem(3),
        out_specs=vmem(1)[0],
        cost_estimate=cost(4 * 16 * BLK * BLK, 3 << 20),
        name="prep",
    )(summary_pos[0, 0], q, k, v)
    *carried, kv = near(True, has, send, k, v)

    got = lax.all_to_all(send, "grp", 0, 0, tiled=True)
    mine = pl.pallas_call(
        pick_kernel,
        out_shape=jax.ShapeDtypeStruct((layers, 64, 128), bf16),
        grid=(1,),
        in_specs=[SMEM, pl.BlockSpec((groups, SUMM, 128), lambda i: (0, HD // SUMM, 0))],
        out_specs=pl.BlockSpec((layers, 64, 128), lambda i: (0, 0, 0)),
        compiler_params=LIMIT,
        name="pick",
    )(where, got)
    both_axes = ("ctx", "grp")
    s00 = lax.all_to_all(mine, both_axes, 0, 0, tiled=True, axis_index_groups=rings)
    s10 = lax.ppermute(s00, "ctx", other_y)
    s01 = lax.ppermute(s00, "grp", other_core)
    s11 = lax.ppermute(s10, "grp", other_core)

    kv, _ = lax.optimization_barrier((kv, s00))
    flat = [t * groups + s for s in range(groups) for t in range(per_group)]
    kv_prev = lax.ppermute(kv, ("ctx", "grp"), list(zip(flat[:-1], flat[1:])))

    partial = pl.pallas_call(
        far_kernel,
        out_shape=jax.ShapeDtypeStruct((groups, SEND, HALF), bf16),
        in_specs=[SMEM] + vmem(5),
        out_specs=vmem(1)[0],
        scratch_shapes=[
            pltpu.VMEM((8, ACC, 512), bf16),
            pltpu.VMEM((8, 512, 128), bf16),
            pltpu.VMEM((groups // 2, 128, 2 * HALF), bf16),
            pltpu.VMEM((8, 512, 2 * HALF), f32),
            pltpu.VMEM((8, 512, 2 * HALF), f32),
        ],
        compiler_params=pltpu.CompilerParams(vmem_limit_bytes=32 << 20),
        cost_estimate=cost(2 * 40 * 1024 * HALF * 256, 3 << 20, 40 * 1024 * HALF),
        name="far",
    )(where, got, s00, s01, s10, s11)
    far = lax.all_to_all(partial, "grp", 0, 0, tiled=True)
    acc, peak = near(False, has, send, kv_prev, *carried)

    out = pl.pallas_call(
        merge_kernel,
        out_shape=jax.ShapeDtypeStruct((BLK, H * HD), bf16),
        in_specs=vmem(3),
        out_specs=vmem(1)[0],
        compiler_params=LIMIT,
        cost_estimate=cost(H * BLK * HD * 8, 3 << 20),
        name="merge",
    )(acc, peak, far)
    return out[None]


def solution(mesh):
    placed = P("grp", "ctx", None)
    return jax.shard_map(
        shards, mesh=mesh, in_specs=(placed,) * 4, out_specs=placed, check_vma=False
    )
```

```python
import functools
import math

import jax
import jax.numpy as jnp
from jax import lax
from jax.experimental import pallas as pl
from jax.experimental.pallas import tpu as pltpu
from jax.sharding import PartitionSpec as P


H = 8
HD = 64
BLK = 512
SUMM = 8
HALF = 256
ACC = 80
SEND = 72
RATE = math.log2(math.e) / math.sqrt(HD)
FLOOR = -1e29
NONE = -1e30
bf16 = jnp.bfloat16
f32 = jnp.float32


def dot(a, b):
    return lax.dot_general(a, b, (((1,), (0,)), ((), ())), preferred_element_type=f32)


def fold(parts, values_t, peak, acc):
    top = peak
    for part in parts:
        top = jnp.maximum(top, part.max(0, keepdims=True))
    weights = [jnp.exp2((part - top) * RATE).astype(bf16) for part in parts]
    rescale = jnp.exp2((peak - top) * RATE)
    acc = acc * rescale + dot(values_t, jnp.concatenate(weights, axis=0))
    return top, acc


def thirds(value):
    high = value.astype(bf16)
    rest = value - high.astype(f32)
    mid = rest.astype(bf16)
    return high, mid, (rest - mid.astype(f32)).astype(bf16)


def prep_kernel(pos_ref, q_ref, k_ref, v_ref, send_ref):
    slot = lax.broadcasted_iota(jnp.int32, (16, BLK), 0)
    token = lax.broadcasted_iota(jnp.int32, (16, BLK), 1)
    wanted = jnp.full((16, BLK), -1, jnp.int32)
    for j in range(SUMM):
        wanted = jnp.where(slot == j, pos_ref[j], wanted)
    pick = jnp.where(token == wanted, 1.0, 0.0).astype(bf16)
    k_rows = dot(pick, k_ref[...])[:SUMM]
    v_rows = dot(pick, v_ref[...])[:SUMM]
    blank = jnp.zeros((SUMM, HALF - 128), f32)
    q_t = q_ref[...].T
    for h in range(H):
        part = slice(h * HD, (h + 1) * HD)
        rows = jnp.concatenate([v_rows[:, part], k_rows[:, part], blank], axis=1).astype(bf16)
        for half in range(2):
            send_ref[2 * h + half, :HD] = q_t[part, half * HALF : (half + 1) * HALF]
            send_ref[2 * h + half, HD:] = rows


def pick_kernel(where_ref, got_ref, out_ref):
    odd = where_ref[1] > 0
    own = [got_ref[i, HD:, :128] for i in range(16)]
    pieces = [jnp.where(odd, own[2 * i + 1], own[2 * i]) for i in range(8)]
    rows = jnp.concatenate(pieces, axis=0)
    for z in range(out_ref.shape[0]):
        out_ref[z] = rows


def near_kernel(own, has_ref, qt_ref, *rest):
    if own:
        k_ref, v_ref, acc_ref, peak_ref, kv_ref, vt_ref = rest
        kv_ref[:, : H * HD] = k_ref[...]
        kv_ref[:, H * HD :] = v_ref[...]
        v_t = v_ref[...].T
    else:
        k_ref, acc_in, peak_in, acc_ref, peak_ref, vt_ref = rest
        v_t = k_ref[:, H * HD :].T
    for h in range(H):
        vt_ref[h, :HD] = v_t[h * HD : (h + 1) * HD]
        vt_ref[h, HD:] = jnp.ones((ACC - HD, BLK), bf16)
    zeros = jnp.zeros((HD, HALF), bf16)
    key_at = lax.broadcasted_iota(jnp.int32, (HALF, HALF), 0)
    query_at = lax.broadcasted_iota(jnp.int32, (HALF, HALF), 1)
    causal = key_at <= query_at
    for h in range(H):
        pair = slice((h // 2) * 128, (h // 2 + 1) * 128)
        for half in range(2):
            cols = slice(half * HALF, (half + 1) * HALF)
            q_t = qt_ref[2 * h + half, :HD]
            q_t = jnp.concatenate([q_t, zeros] if h % 2 == 0 else [zeros, q_t], axis=0)
            if own:
                count = (half + 1) * HALF
                parts = [dot(k_ref[i : i + HALF, pair], q_t) for i in range(0, count, HALF)]
                parts[-1] = jnp.where(causal, parts[-1], NONE)
                peak = jnp.full((1, HALF), FLOOR, f32)
                acc = jnp.zeros((ACC, HALF), f32)
            else:
                count = BLK
                parts = [dot(k_ref[i : i + HALF, pair], q_t) for i in range(0, count, HALF)]
                peak = peak_in[h, :1, cols]
                acc = acc_in[h, :, cols]
            new_peak, new_acc = fold(parts, vt_ref[h, :, :count], peak, acc)
            if not own:
                has = has_ref[0] > 0
                new_peak = jnp.where(has, new_peak, peak)
                new_acc = jnp.where(has, new_acc, acc)
            acc_ref[h, :, cols] = new_acc
            peak_ref[h, :, cols] = jnp.broadcast_to(new_peak, (8, HALF))


def far_kernel(where_ref, q_ref, s00_ref, s01_ref, s10_ref, s11_ref, out_ref, vt_ref, k_ref, qt_ref, even_ref, odd_ref):
    c = where_ref[0]
    half = where_ref[1]
    y = c // 16
    sets = (s00_ref, s01_ref, s10_ref, s11_ref)
    part = 128
    tile = 4 * part
    wide = 2 * HALF
    lane = lax.broadcasted_iota(jnp.int32, (part, 128), 1)
    layer = lax.broadcasted_iota(jnp.int32, (part, 128), 0) // SUMM
    low = lane < HD
    shift = jnp.where(lane < 16, 32 * lane, 1 << 20)
    ages = []
    for hh in range(2):
        turned = jnp.where((half ^ hh) > 0, layer ^ 8, layer)
        ages.append(turned - shift)
    for gg in range(8):
        for i, ref in enumerate(sets):
            at = slice(i * part, (i + 1) * part)
            rows = ref[:, gg * SUMM : (gg + 1) * SUMM].reshape(part, 128)
            start = 64 * gg + 32 * (half ^ (i % 2)) + 16 * (y ^ (i // 2))
            bias = jnp.where(ages[i % 2] <= c - 2 - start, 0.0, NONE).astype(bf16)
            k_ref[gg, at] = jnp.where(low, bias, rows)
            vt_ref[gg, :, at] = rows.T[:ACC]
        vt_ref[gg, HD:] = jnp.ones((ACC - HD, tile), bf16)
    at = lax.broadcasted_iota(jnp.int32, (HD, HALF), 0)
    for g in range(16):
        one_hot = jnp.where(at == g, 1.0, 0.0).astype(bf16)
        cols = slice((g % 2) * HALF, (g % 2 + 1) * HALF)
        qt_ref[g // 2, :, cols] = jnp.concatenate([one_hot, q_ref[g, :HD]], axis=0)

    def scores(pair, first, count, buf, peak):
        for j in range(count):
            for i in range(0, tile, 256):
                piece = dot(k_ref[first + j, i : i + 256], qt_ref[pair])
                buf[first + j, i : i + 256] = piece
                peak = jnp.maximum(peak, piece.reshape(32, 8, wide).max(0))
        return peak

    def values(first, count, buf, top, acc):
        weights = [
            jnp.exp2((buf[first + j, i : i + 256] - top) * RATE).astype(bf16)
            for j in range(count)
            for i in range(0, tile, 256)
        ]
        rows = [vt_ref[first + j] for j in range(count)]
        return acc + dot(jnp.concatenate(rows, axis=1), jnp.concatenate(weights, axis=0))

    def finish(pair, top, acc):
        total = acc[HD : HD + 1]
        some = total > 0.0
        safe = jnp.where(some, total, 1.0)
        result = (acc[:HD] * (1.0 / safe)).astype(bf16)
        level = jnp.where(some, top * RATE + jnp.log2(safe), NONE)
        stats = jnp.concatenate([*thirds(level), jnp.zeros((SEND - HD - 3, wide), bf16)], axis=0)
        for j in range(2):
            cols = slice(j * HALF, (j + 1) * HALF)
            out_ref[2 * pair + j, :HD] = result[:, cols]
            out_ref[2 * pair + j, HD:] = stats[:, cols]

    floor = jnp.full((8, wide), FLOOR, f32)
    empty = jnp.zeros((ACC, wide), f32)

    def turn(pair, tiles, this, other, peak):
        top = peak.max(0, keepdims=True)
        later = pair + 1

        def both(p, carry):
            acc, ahead = carry
            ahead = scores(later, 2 * p, 2, other, ahead)
            acc = values(2 * p, 2, this, top, acc)
            return acc, ahead

        return later, top, *lax.fori_loop(0, tiles, both, (empty, floor))

    def even(i, peak):
        later, top, acc, ahead = turn(2 * i, i, even_ref, odd_ref, peak)
        ahead = scores(later, 2 * i, 2, odd_ref, ahead)
        acc = values(2 * i, 1, even_ref, top, acc)
        finish(2 * i, top, acc)
        return ahead

    def odd(i, peak):
        later, top, acc, ahead = turn(2 * i + 1, i + 1, odd_ref, even_ref, peak)
        ahead = scores(later, 2 * i + 2, 1, even_ref, ahead)
        finish(2 * i + 1, top, acc)
        return ahead

    peak = scores(0, 0, 1, even_ref, floor)
    peak = lax.fori_loop(0, 3, lambda i, peak: odd(i, even(i, peak)), peak)
    top = even(3, peak).max(0, keepdims=True)
    finish(7, top, lax.fori_loop(0, 2, lambda p, acc: values(4 * p, 4, odd_ref, top, acc), empty))


def merge_kernel(acc_ref, peak_ref, far_ref, out_ref):
    for h in range(H):
        columns = []
        for half in range(2):
            cols = slice(half * HALF, (half + 1) * HALF)
            far = far_ref[2 * h + half]
            stats = far[HD:].astype(f32)
            level = stats[0:1] + (stats[1:2] + stats[2:3])
            near = peak_ref[h, :1, cols] * RATE
            top = jnp.maximum(near, level)
            near = jnp.exp2(near - top)
            level = jnp.exp2(level - top)
            total = acc_ref[h, HD : HD + 1, cols] * near + level
            result = acc_ref[h, :HD, cols] * (near / total) + far[:HD].astype(f32) * (level / total)
            columns.append(result)
        wide = jnp.concatenate(columns, axis=1).astype(bf16)
        if h % 2 == 0:
            first = wide
        else:
            both = jnp.concatenate([first, wide], axis=0)
            out_ref[:, (h // 2) * 128 : (h // 2 + 1) * 128] = both.T


def vmem(count):
    return [pl.BlockSpec(memory_space=pltpu.VMEM)] * count


SMEM = pl.BlockSpec(memory_space=pltpu.SMEM)


LIMIT = pltpu.CompilerParams(vmem_limit_bytes=24 << 20)


def cost(flops, size, exps=0):
    return pl.CostEstimate(flops=flops, bytes_accessed=size, transcendentals=exps)


def near(own, has, *args):
    shapes = (
        jax.ShapeDtypeStruct((H, ACC, BLK), f32),
        jax.ShapeDtypeStruct((H, 8, BLK), f32),
    )
    if own:
        shapes += (jax.ShapeDtypeStruct((BLK, 2 * H * HD), bf16),)
    return pl.pallas_call(
        functools.partial(near_kernel, own),
        out_shape=shapes,
        in_specs=[SMEM] + vmem(len(args)),
        out_specs=tuple(vmem(len(shapes))),
        scratch_shapes=[pltpu.VMEM((H, ACC, BLK), bf16)],
        compiler_params=LIMIT,
        cost_estimate=cost(2 * H * BLK * BLK * 256, 4 << 20, H * BLK * BLK),
        name="near_own" if own else "near_prev",
    )(has, *args)


def shards(queries, keys, values, summary_pos):
    c = lax.axis_index("ctx")
    g = lax.axis_index("grp")
    groups, per_group = lax.axis_size("grp"), lax.axis_size("ctx")
    layers = per_group // 2
    rings = [
        [(y * layers + (z + layers // 2 * (i % 2)) % layers) * groups + i for z in range(layers)]
        for y in range(2)
        for i in range(groups)
    ]
    other_y = [(i, (i + layers) % per_group) for i in range(per_group)]
    other_core = [(i, i ^ 1) for i in range(groups)]
    q, k, v = queries[0], keys[0], values[0]

    where = jnp.stack([c, g % 2]).astype(jnp.int32)
    has = jnp.where(c + g > 0, 1, 0).astype(jnp.int32)[None]
    send = pl.pallas_call(
        prep_kernel,
        out_shape=jax.ShapeDtypeStruct((groups, SEND, HALF), bf16),
        in_specs=[SMEM] + vmem(3),
        out_specs=vmem(1)[0],
        cost_estimate=cost(4 * 16 * BLK * BLK, 3 << 20),
        name="prep",
    )(summary_pos[0, 0], q, k, v)
    *carried, kv = near(True, has, send, k, v)

    got = lax.all_to_all(send, "grp", 0, 0, tiled=True)
    mine = pl.pallas_call(
        pick_kernel,
        out_shape=jax.ShapeDtypeStruct((layers, 64, 128), bf16),
        in_specs=[SMEM] + vmem(1),
        out_specs=vmem(1)[0],
        compiler_params=LIMIT,
        name="pick",
    )(where, got)
    both_axes = ("ctx", "grp")
    s00 = lax.all_to_all(mine, both_axes, 0, 0, tiled=True, axis_index_groups=rings)
    s10 = lax.ppermute(s00, "ctx", other_y)
    s01 = lax.ppermute(s00, "grp", other_core)
    s11 = lax.ppermute(s10, "grp", other_core)

    kv, _ = lax.optimization_barrier((kv, s00))
    flat = [t * groups + s for s in range(groups) for t in range(per_group)]
    kv_prev = lax.ppermute(kv, ("ctx", "grp"), list(zip(flat[:-1], flat[1:])))

    partial = pl.pallas_call(
        far_kernel,
        out_shape=jax.ShapeDtypeStruct((groups, SEND, HALF), bf16),
        in_specs=[SMEM] + vmem(5),
        out_specs=vmem(1)[0],
        scratch_shapes=[
            pltpu.VMEM((8, ACC, 512), bf16),
            pltpu.VMEM((8, 512, 128), bf16),
            pltpu.VMEM((groups // 2, 128, 2 * HALF), bf16),
            pltpu.VMEM((8, 512, 2 * HALF), f32),
            pltpu.VMEM((8, 512, 2 * HALF), f32),
        ],
        compiler_params=pltpu.CompilerParams(vmem_limit_bytes=32 << 20),
        cost_estimate=cost(2 * 40 * 1024 * HALF * 256, 3 << 20, 40 * 1024 * HALF),
        name="far",
    )(where, got, s00, s01, s10, s11)
    far = lax.all_to_all(partial, "grp", 0, 0, tiled=True)
    acc, peak = near(False, has, send, kv_prev, *carried)

    out = pl.pallas_call(
        merge_kernel,
        out_shape=jax.ShapeDtypeStruct((BLK, H * HD), bf16),
        in_specs=vmem(3),
        out_specs=vmem(1)[0],
        compiler_params=LIMIT,
        cost_estimate=cost(H * BLK * HD * 8, 3 << 20),
        name="merge",
    )(acc, peak, far)
    return out[None]


def solution(mesh):
    placed = P("grp", "ctx", None)
    return jax.shard_map(
        shards, mesh=mesh, in_specs=(placed,) * 4, out_specs=placed, check_vma=False
    )
```
